32 devices in a mesh: fsdp: 2 (over x), context: 4 (over z), tensor: 4 (over y, core).
Axes of the slice: x: 2, y: 2, z: 4, core: 2. Of those that a mesh axis runs over, the one named last changes fastest.
Arguments:
- tokens: bfloat16 [4096, 960], P(('fsdp', 'context', 'tensor')), may hold values from -6 to 6
- positions: int32 [2, 2048], P('fsdp'), may hold values from 0 to 2047, as said below
- cotangent: bfloat16 [4096, 960], P(('fsdp', 'context', 'tensor')), may hold values from -6 to 6
- attn_gain: bfloat16 [960], P('fsdp'), may hold values from 0.099609375 to 1.8984375
- query_weight: bfloat16 [960, 960], P('fsdp'), as said below
- key_weight: bfloat16 [960, 320], P('fsdp'), as said below
- value_weight: bfloat16 [960, 320], P('fsdp'), may hold values from -0.1875 to 0.1875
- out_weight: bfloat16 [960, 960], P('fsdp'), may hold values from -1 to 1
- mlp_gain: bfloat16 [960], P('fsdp'), may hold values from 0.099609375 to 1.8984375
- gate_weight: bfloat16 [960, 2560], P('fsdp', 'tensor'), may hold values from -0.1875 to 0.1875
- up_weight: bfloat16 [960, 2560], P('fsdp', 'tensor'), may hold values from -0.1875 to 0.1875
- down_weight: bfloat16 [960, 2560], P('fsdp', 'tensor'), may hold values from -0.125 to 0.125
Outputs:
- output: bfloat16 [4096, 960], P(('fsdp', 'context', 'tensor'))
- input_grad: float32 [4096, 960], P(('fsdp', 'context', 'tensor'))
- attn_gain_grad: float32 [960], P('fsdp')
- query_grad: float32 [960, 960], P('fsdp')
- key_grad: float32 [960, 320], P('fsdp')
- value_grad: float32 [960, 320], P('fsdp')
- out_grad: float32 [960, 960], P('fsdp')
- mlp_gain_grad: float32 [960], P('fsdp')
- gate_grad: float32 [960, 2560], P('fsdp', 'tensor')
- up_grad: float32 [960, 2560], P('fsdp', 'tensor')
- down_grad: float32 [960, 2560], P('fsdp', 'tensor')
The draws below stay inside these ranges and needn't reach their ends.
Inputs may be any that keep to these rules, and one draw needn't show every extreme that they name: Each sequence holds every position from 0 once; its rows form blocks of 64 rows of consecutive rising positions, each block starting at a multiple of 64. `query_weight`: entries of either sign. `key_weight`: entries of either sign.
All inputs are finite; a program needn't handle non-finite values.
Results may differ from the reference program's by a relative error of at most 0.025.
The reference program's roundings to bfloat16 on the way (of `normed_one`, `value`, `probs`, `attended`, `normed_two`, `act`, `d_attended` and `d_scores`) count: a program that leaves them out, or rounds other values in their place, can miss the bound.
Values may be sent and summed in bfloat16 or wider, within the bound.
A program may use at most 128 MiB of HBM per device.

```python
import jax
import jax.numpy as jnp
from jax import lax

D = 960
HEADS = 15
KV_HEADS = 5
HD = 64
FF = 2560
STRETCH = 64
SEQ_LEN = 2048
SEQS = 2
TOKENS = 4096


def draw_positions(key, part):
    slots = SEQ_LEN // STRETCH
    orders = jax.vmap(lambda single: jax.random.permutation(single, slots))(jax.random.split(key, SEQS))
    offsets = jnp.arange(STRETCH, dtype=jnp.int32)
    places = orders.astype(jnp.int32)[:, :, None] * STRETCH + offsets[None, None, :]
    return places.reshape(SEQS, SEQ_LEN).astype(jnp.int32)


def projection_draw(key, columns):
    values = jax.random.normal(key, (D, columns), jnp.float32) * D ** (-0.5)
    return values.astype(jnp.bfloat16)


def draw_query_weight(key, part):
    return projection_draw(jax.random.fold_in(key, 11), HEADS * HD)


def draw_key_weight(key, part):
    return projection_draw(jax.random.fold_in(key, 23), KV_HEADS * HD)


def levels(key, dims, pieces, least, largest):
    factor_of, own = 1.0, jax.random.fold_in(key, 6)
    for axis_at, parts in pieces:
        draws = jnp.exp(jax.random.uniform(jax.random.fold_in(own, axis_at), (parts,), jnp.float32, least / len(pieces), largest / len(pieces)))
        factor_of = factor_of * jnp.repeat(draws, dims[axis_at] // parts).reshape([-1 if axis == axis_at else 1 for axis in range(len(dims))])
    return factor_of


def scatter_about(key, extent, width, bound, cuts=(), held_as=jnp.bfloat16):
    array = jax.random.normal(key, extent, jnp.float32) * width
    if len(cuts) > 0:
        array = levels(key, extent, cuts, -0.22, 0.18) * array
    return jnp.clip(array, min=-bound, max=bound).astype(held_as)


def setup_inputs(seed: int = 0) -> dict:
    key_of = jax.random.split(jax.random.key(seed), 13)
    tokens = scatter_about(key_of[0], (TOKENS, D), 1.0, 6.0, ((0, 32),))
    positions = draw_positions(jax.random.fold_in(key_of[12], 71), 0)
    cotangent = scatter_about(key_of[2], (TOKENS, D), 1.0, 6.0, ((0, 32),))
    attn_gain = jnp.clip(1.0 + 0.18 * jax.random.normal(key_of[3], (D,), jnp.float32), 0.099609375, 1.8984375).astype(jnp.bfloat16)
    query_weight = draw_query_weight(jax.random.fold_in(key_of[12], 71), 0)
    key_weight = draw_key_weight(jax.random.fold_in(key_of[12], 71), 0)
    value_weight = scatter_about(key_of[6], (D, KV_HEADS * HD), D ** -0.5, 0.1875, ((0, 2),))
    out_weight = scatter_about(key_of[7], (HEADS * HD, D), (HEADS * HD // 32) ** -0.5, 1.0, ((0, 2),))
    mlp_gain = jnp.clip(1.0 + 0.18 * jax.random.normal(key_of[8], (D,), jnp.float32), 0.099609375, 1.8984375).astype(jnp.bfloat16)
    gate_weight = scatter_about(key_of[9], (D, FF), D ** -0.5, 0.1875, ((0, 2), (1, 4)))
    up_weight = scatter_about(key_of[10], (D, FF), D ** -0.5, 0.1875, ((0, 2), (1, 4)))
    down_weight = scatter_about(key_of[11], (D, FF), FF ** -0.5, 0.125, ((0, 2), (1, 4)))
    return {"tokens": tokens, "positions": positions, "cotangent": cotangent, "attn_gain": attn_gain, "query_weight": query_weight, "key_weight": key_weight, "value_weight": value_weight, "out_weight": out_weight, "mlp_gain": mlp_gain, "gate_weight": gate_weight, "up_weight": up_weight, "down_weight": down_weight}


EPS = 1e-05
THETA = 100000.0
NEG = -1e+30
ROWS_MATCH = (((0,), (0,)), ((), ()))
COLS_MATCH = (((1,), (1,)), ((), ()))

def norm_scale(values):
    return lax.rsqrt(lax.optimization_barrier(jnp.mean(values * values, axis=1, keepdims=True)) + EPS)

def norm_back(grad, hat, scale, gain):
    weighted = grad * gain
    return scale * (weighted - hat * lax.optimization_barrier(jnp.mean(weighted * hat, axis=1, keepdims=True)))

def rotary_tables(places):
    half = HD // 2
    freq = THETA ** (-2.0 * jnp.arange(half, dtype=jnp.float32) / HD)
    angle = places.astype(jnp.float32)[:, None] * freq[None, :]
    cosine = jnp.concatenate([jnp.cos(angle), jnp.cos(angle)], axis=1)[:, None, :]
    sine = jnp.concatenate([jnp.sin(angle), jnp.sin(angle)], axis=1)[:, None, :]
    return (cosine, sine)

def rotate(values, cosine, sine):
    half = values.shape[-1] // 2
    turned = jnp.concatenate([-values[..., half:], values[..., :half]], axis=-1)
    return values * cosine + turned * sine

def unrotate(values, cosine, sine):
    half = values.shape[-1] // 2
    scaled = values * sine
    return values * cosine + jnp.concatenate([scaled[..., half:], -scaled[..., :half]], axis=-1)

def masked_scores(q_block, block_places, keys, places):
    factor = HD ** (-0.5)
    scores = jnp.einsum('qgrd,kgd->grqk', q_block.astype(jnp.float32), keys.astype(jnp.float32)) * factor
    mask = places[None, :] <= block_places[:, None]
    return (jnp.where(mask, scores, NEG), mask)

def one_sequence(seq_tokens, places, seq_cot, weights):
    attn_gain, query_weight, key_weight, value_weight, out_weight, mlp_gain, gate_weight, up_weight, down_weight = weights
    length = seq_tokens.shape[0]
    groups = HEADS // KV_HEADS
    block = min(512, length)
    count = length // block
    factor = HD ** (-0.5)
    inputs = seq_tokens.astype(jnp.float32)
    first_scale = norm_scale(inputs)
    gain_one = attn_gain.astype(jnp.float32)
    normed_one = (inputs * first_scale * gain_one).astype(jnp.bfloat16)
    cosine, sine = rotary_tables(places)
    query = jnp.dot(normed_one, query_weight, preferred_element_type=jnp.float32).reshape(length, HEADS, HD)
    key_raw = jnp.dot(normed_one, key_weight, preferred_element_type=jnp.float32).reshape(length, KV_HEADS, HD)
    value = jnp.dot(normed_one, value_weight, preferred_element_type=jnp.float32).astype(jnp.bfloat16).reshape(length, KV_HEADS, HD)
    q_rot = rotate(query, cosine, sine).astype(jnp.bfloat16).reshape(length, KV_HEADS, groups, HD)
    k_rot = rotate(key_raw, cosine, sine).astype(jnp.bfloat16)

    def forward_block(index):
        start = index * block
        q_block = lax.dynamic_slice_in_dim(q_rot, start, block, 0)
        block_places = lax.dynamic_slice_in_dim(places, start, block, 0)
        scores, mask = masked_scores(q_block, block_places, k_rot, places)
        peak = lax.optimization_barrier(jnp.max(scores, axis=-1, keepdims=True))
        total = jnp.log(lax.optimization_barrier(jnp.sum(jnp.exp(scores - peak), axis=-1, keepdims=True))) + peak
        probs = jnp.where(mask, jnp.exp(scores - total), 0.0).astype(jnp.bfloat16)
        mixed = jnp.einsum('grqk,kgd->qgrd', probs.astype(jnp.float32), value.astype(jnp.float32))
        return (mixed, total[..., 0])
    mixed, totals = lax.map(forward_block, jnp.arange(count, dtype=jnp.int32))
    attended = mixed.reshape(length, HEADS * HD).astype(jnp.bfloat16)
    residual = inputs + jnp.dot(attended, out_weight, preferred_element_type=jnp.float32)
    second_scale = norm_scale(residual)
    gain_two = mlp_gain.astype(jnp.float32)
    normed_two = (residual * second_scale * gain_two).astype(jnp.bfloat16)
    gate = jnp.dot(normed_two, gate_weight, preferred_element_type=jnp.float32)
    up = jnp.dot(normed_two, up_weight, preferred_element_type=jnp.float32)
    act = (jax.nn.silu(gate) * up).astype(jnp.bfloat16)
    feed = lax.dot_general(act, down_weight, COLS_MATCH, preferred_element_type=jnp.float32)
    output = (residual + feed).astype(jnp.bfloat16)
    d_act = jnp.dot(seq_cot, down_weight, preferred_element_type=jnp.float32)
    down_grad = lax.dot_general(seq_cot, act, ROWS_MATCH, preferred_element_type=jnp.float32)
    sig = jax.nn.sigmoid(gate)
    d_gate = (d_act * up * sig * (1.0 + gate * (1.0 - sig))).astype(jnp.bfloat16)
    d_up = (d_act * gate * sig).astype(jnp.bfloat16)
    gate_grad = lax.dot_general(normed_two, d_gate, ROWS_MATCH, preferred_element_type=jnp.float32)
    up_grad = lax.dot_general(normed_two, d_up, ROWS_MATCH, preferred_element_type=jnp.float32)
    d_normed_two = lax.dot_general(d_gate, gate_weight, COLS_MATCH, preferred_element_type=jnp.float32)
    d_normed_two = d_normed_two + lax.dot_general(d_up, up_weight, COLS_MATCH, preferred_element_type=jnp.float32)
    hat_two = residual * second_scale
    mlp_gain_grad = lax.optimization_barrier(jnp.sum(d_normed_two * hat_two, axis=0))
    d_residual = seq_cot.astype(jnp.float32) + norm_back(d_normed_two, hat_two, second_scale, gain_two)
    residual_round = d_residual.astype(jnp.bfloat16)
    out_grad = lax.dot_general(attended, residual_round, ROWS_MATCH, preferred_element_type=jnp.float32)
    d_attended = lax.dot_general(residual_round, out_weight, COLS_MATCH, preferred_element_type=jnp.float32).astype(jnp.bfloat16)
    delta = lax.optimization_barrier(jnp.sum((d_attended.astype(jnp.float32) * attended.astype(jnp.float32)).reshape(length, KV_HEADS, groups, HD), axis=-1))
    d_att4 = d_attended.reshape(length, KV_HEADS, groups, HD)

    def backward_block(carry, index):
        key_sum, value_sum = carry
        start = index * block
        q_block = lax.dynamic_slice_in_dim(q_rot, start, block, 0)
        block_places = lax.dynamic_slice_in_dim(places, start, block, 0)
        d_block = lax.dynamic_slice_in_dim(d_att4, start, block, 0)
        delta_block = jnp.transpose(lax.dynamic_slice_in_dim(delta, start, block, 0), (1, 2, 0))
        scores, mask = masked_scores(q_block, block_places, k_rot, places)
        probs = jnp.where(mask, jnp.exp(scores - totals[index][..., None]), 0.0)
        d_probs = jnp.einsum('qgrd,kgd->grqk', d_block.astype(jnp.float32), value.astype(jnp.float32))
        d_scores = (probs * (d_probs - delta_block[..., None]) * factor).astype(jnp.bfloat16)
        d_query = jnp.einsum('grqk,kgd->qgrd', d_scores.astype(jnp.float32), k_rot.astype(jnp.float32))
        key_sum = key_sum + jnp.einsum('grqk,qgrd->kgd', d_scores.astype(jnp.float32), q_block.astype(jnp.float32))
        value_sum = value_sum + jnp.einsum('grqk,qgrd->kgd', probs.astype(jnp.bfloat16).astype(jnp.float32), d_block.astype(jnp.float32))
        return ((key_sum, value_sum), d_query)
    empty = jnp.zeros((length, KV_HEADS, HD), jnp.float32)
    (d_key, d_value), d_query = lax.scan(backward_block, (empty, empty), jnp.arange(count, dtype=jnp.int32))
    dq_rot = unrotate(d_query.reshape(length, HEADS, HD), cosine, sine).astype(jnp.bfloat16).reshape(length, HEADS * HD)
    dk_rot = unrotate(d_key, cosine, sine).astype(jnp.bfloat16).reshape(length, KV_HEADS * HD)
    dv_round = d_value.astype(jnp.bfloat16).reshape(length, KV_HEADS * HD)
    query_grad = lax.dot_general(normed_one, dq_rot, ROWS_MATCH, preferred_element_type=jnp.float32)
    key_grad = lax.dot_general(normed_one, dk_rot, ROWS_MATCH, preferred_element_type=jnp.float32)
    value_grad = lax.dot_general(normed_one, dv_round, ROWS_MATCH, preferred_element_type=jnp.float32)
    d_normed_one = lax.dot_general(dq_rot, query_weight, COLS_MATCH, preferred_element_type=jnp.float32)
    d_normed_one = d_normed_one + lax.dot_general(dk_rot, key_weight, COLS_MATCH, preferred_element_type=jnp.float32)
    d_normed_one = d_normed_one + lax.dot_general(dv_round, value_weight, COLS_MATCH, preferred_element_type=jnp.float32)
    hat_one = inputs * first_scale
    attn_gain_grad = lax.optimization_barrier(jnp.sum(d_normed_one * hat_one, axis=0))
    input_grad = d_residual + norm_back(d_normed_one, hat_one, first_scale, gain_one)
    grads = (attn_gain_grad, query_grad, key_grad, value_grad, out_grad, mlp_gain_grad, gate_grad, up_grad, down_grad)
    return (output, input_grad, grads)

def reference(tokens, positions, cotangent, attn_gain, query_weight, key_weight, value_weight, out_weight, mlp_gain, gate_weight, up_weight, down_weight):
    weights = (attn_gain, query_weight, key_weight, value_weight, out_weight, mlp_gain, gate_weight, up_weight, down_weight)
    seq_tokens = tokens.reshape(SEQS, SEQ_LEN, D)
    seq_cot = cotangent.reshape(SEQS, SEQ_LEN, D)
    zeros = tuple((jnp.zeros(weight.shape, jnp.float32) for weight in weights))

    def step(carry, item):
        rows_in, places, rows_cot = item
        output, input_grad, grads = one_sequence(rows_in, places, rows_cot, weights)
        return (tuple((left + right for left, right in zip(carry, grads))), (output, input_grad))
    sums, (outputs, input_grads) = lax.scan(step, zeros, (seq_tokens, positions, seq_cot))
    return (outputs.reshape(TOKENS, D), input_grads.reshape(TOKENS, D), sums[0], sums[1], sums[2], sums[3], sums[4], sums[5], sums[6], sums[7], sums[8])
```

```python
import jax
import jax.numpy as jnp
from jax import lax
from jax.experimental import pallas as pl
from jax.experimental.pallas import tpu as pltpu
from jax.sharding import PartitionSpec as P

HEADS = 15
KV_HEADS = 5
HD = 64


EPS = 1e-05
THETA = 100000.0
NEG = -1e30
ROWS_MATCH = (((0,), (0,)), ((), ()))
COLS_MATCH = (((1,), (1,)), ((), ()))


def norm_scale(values):
    return lax.rsqrt(jnp.mean(values * values, axis=1, keepdims=True) + EPS)


def norm_back(grad, hat, scale, gain):
    weighted = grad * gain
    return scale * (weighted - hat * jnp.mean(weighted * hat, axis=1, keepdims=True))


def rotary_tables(places):
    half = HD // 2
    freq = THETA ** (-2.0 * jnp.arange(half, dtype=jnp.float32) / HD)
    angle = places.astype(jnp.float32)[:, None] * freq[None, :]
    cosine = jnp.concatenate([jnp.cos(angle), jnp.cos(angle)], axis=1)[:, None, :]
    sine = jnp.concatenate([jnp.sin(angle), jnp.sin(angle)], axis=1)[:, None, :]
    return (cosine, sine)


def rotate(values, cosine, sine):
    half = values.shape[-1] // 2
    turned = jnp.concatenate([-values[..., half:], values[..., :half]], axis=-1)
    return values * cosine + turned * sine


def unrotate(values, cosine, sine):
    half = values.shape[-1] // 2
    scaled = values * sine
    return values * cosine + jnp.concatenate([scaled[..., half:], -scaled[..., :half]], axis=-1)


KEYS_MATCH = (((0,), (0,)), ((), ()))


def masked_scores(kv, queries, key_places, own_places):
    scores = lax.dot_general(
        kv, queries, COLS_MATCH, preferred_element_type=jnp.float32
    ) * HD ** (-0.5)
    return jnp.where(key_places <= own_places, scores, NEG)


def forward_kernel(key_places_ref, own_places_ref, q_ref, kv_ref, out_ref, lse_ref):
    owners, _, block, width = kv_ref.shape
    kv = kv_ref[...].reshape(owners * block, width)
    scores = masked_scores(kv, q_ref[0], key_places_ref[...], own_places_ref[...])
    peak = jnp.max(scores, axis=0, keepdims=True)
    weights = jnp.exp(scores - peak)
    summed = jnp.sum(weights, axis=0, keepdims=True)
    mixed = lax.dot_general(
        kv, weights.astype(jnp.bfloat16), KEYS_MATCH, preferred_element_type=jnp.float32
    )
    out_ref[0] = (mixed[HD:] / summed).astype(jnp.bfloat16)
    lse_ref[0] = peak + jnp.log(summed)


def backward_kernel(
    key_places_ref, own_places_ref, q_ref, d_att_ref, kv_ref, lse_ref, delta_ref, dq_ref, dkv_ref
):
    owners, _, block, width = kv_ref.shape
    kv = kv_ref[...].reshape(owners * block, width)
    scores = masked_scores(kv, q_ref[0], key_places_ref[...], own_places_ref[...])
    probs = jnp.exp(scores - lse_ref[0])
    d_probs = lax.dot_general(kv, d_att_ref[0], COLS_MATCH, preferred_element_type=jnp.float32)
    d_scores = (probs * (d_probs - delta_ref[0]) * HD ** (-0.5)).astype(jnp.bfloat16)
    dq = lax.dot_general(kv, d_scores, KEYS_MATCH, preferred_element_type=jnp.float32)
    dq_ref[0] = dq[:HD]
    d_kv = jnp.dot(d_scores, q_ref[0], preferred_element_type=jnp.float32)
    d_kv = d_kv + jnp.dot(
        probs.astype(jnp.bfloat16), d_att_ref[0], preferred_element_type=jnp.float32
    )
    dkv_ref[...] = d_kv.astype(jnp.bfloat16).reshape(owners, 1, block, width)


def attention_specs(all_kv, lanes):
    owners, _, block, width = all_kv.shape
    total = owners * block
    places = pl.BlockSpec((total, 1), lambda g: (0, 0))
    own = pl.BlockSpec((1, lanes), lambda g: (0, 0))
    queries = pl.BlockSpec((1, lanes, width), lambda g: (g, 0, 0))
    kv = pl.BlockSpec((owners, 1, block, width), lambda g: (0, g, 0, 0))
    row = pl.BlockSpec((1, 1, lanes), lambda g: (g, 0, 0))
    turned = pl.BlockSpec((1, HD, lanes), lambda g: (g, 0, 0))
    cost = KV_HEADS * total * lanes
    return places, own, queries, kv, row, turned, cost


def attend_forward(key_places, own_lanes, q_pad, all_kv):
    lanes = q_pad.shape[1]
    places, own, queries, kv, row, turned, cost = attention_specs(all_kv, lanes)
    return pl.pallas_call(
        forward_kernel,
        grid=(KV_HEADS,),
        in_specs=[places, own, queries, kv],
        out_specs=[turned, row],
        out_shape=[
            jax.ShapeDtypeStruct((KV_HEADS, HD, lanes), jnp.bfloat16),
            jax.ShapeDtypeStruct((KV_HEADS, 1, lanes), jnp.float32),
        ],
        cost_estimate=pl.CostEstimate(
            flops=8 * HD * cost, bytes_accessed=2 * all_kv.size, transcendentals=cost
        ),
    )(key_places, own_lanes, q_pad, all_kv)


def attend_backward(key_places, own_lanes, q_pad, d_att_pad, all_kv, totals, delta):
    lanes = q_pad.shape[1]
    places, own, queries, kv, row, turned, cost = attention_specs(all_kv, lanes)
    return pl.pallas_call(
        backward_kernel,
        grid=(KV_HEADS,),
        in_specs=[places, own, queries, queries, kv, row, row],
        out_specs=[turned, kv],
        out_shape=[
            jax.ShapeDtypeStruct((KV_HEADS, HD, lanes), jnp.float32),
            jax.ShapeDtypeStruct(all_kv.shape, jnp.bfloat16),
        ],
        cost_estimate=pl.CostEstimate(
            flops=20 * HD * cost, bytes_accessed=4 * all_kv.size, transcendentals=cost
        ),
    )(key_places, own_lanes, q_pad, d_att_pad, all_kv, totals, delta)


def per_device(
    tokens,
    positions,
    cotangent,
    attn_gain,
    query_weight,
    key_weight,
    value_weight,
    out_weight,
    mlp_gain,
    gate_weight,
    up_weight,
    down_weight,
):
    rows, width = tokens.shape
    groups = HEADS // KV_HEADS
    lanes = groups * rows
    q_cols, kv_cols = query_weight.shape[1], key_weight.shape[1]
    qkv_cols = q_cols + 2 * kv_cols
    hidden = gate_weight.shape[1]
    place = lax.axis_index(("context", "tensor"))
    sequence_places = positions[0]
    own_places = lax.dynamic_slice_in_dim(sequence_places, place * rows, rows, 0)
    key_places = sequence_places[:, None]
    own_lanes = jnp.tile(own_places, groups)[None, :]

    first_pack = lax.all_gather(
        jnp.concatenate(
            [query_weight, key_weight, value_weight, attn_gain[:, None], mlp_gain[:, None]], axis=1
        ),
        "fsdp",
        axis=0,
        tiled=True,
    )
    qkv_full = first_pack[:, :qkv_cols]
    gain_one = first_pack[:, qkv_cols].astype(jnp.float32)
    gain_two = first_pack[:, qkv_cols + 1].astype(jnp.float32)
    second_pack = lax.all_gather(
        jnp.concatenate([gate_weight, up_weight, down_weight, out_weight], axis=1),
        "fsdp",
        axis=0,
        tiled=True,
    )
    gate_up_full = second_pack[:, : 2 * hidden]
    down_full = second_pack[:, 2 * hidden : 3 * hidden]
    out_full = second_pack[:, 3 * hidden :]

    inputs = tokens.astype(jnp.float32)
    first_scale = norm_scale(inputs)
    normed_one = (inputs * first_scale * gain_one).astype(jnp.bfloat16)
    cosine, sine = rotary_tables(own_places)
    qkv = jnp.dot(normed_one, qkv_full, preferred_element_type=jnp.float32)
    query = qkv[:, :q_cols].reshape(rows, HEADS, HD)
    key_raw = qkv[:, q_cols : q_cols + kv_cols].reshape(rows, KV_HEADS, HD)
    value = qkv[:, q_cols + kv_cols :].reshape(rows, KV_HEADS, HD).astype(jnp.bfloat16)
    q_rot = rotate(query, cosine, sine).astype(jnp.bfloat16)
    k_rot = rotate(key_raw, cosine, sine).astype(jnp.bfloat16)
    own_kv = jnp.transpose(jnp.concatenate([k_rot, value], axis=2), (1, 0, 2))
    all_kv = lax.all_gather(own_kv, ("context", "tensor"), axis=0)
    q_group = jnp.transpose(q_rot, (1, 0, 2)).reshape(KV_HEADS, lanes, HD)
    q_pad = jnp.pad(q_group, ((0, 0), (0, 0), (0, HD)))
    turned, totals = attend_forward(key_places, own_lanes, q_pad, all_kv)
    attended = jnp.transpose(
        turned.reshape(KV_HEADS, HD, groups, rows), (3, 0, 2, 1)
    ).reshape(rows, HEADS * HD)

    residual = inputs + jnp.dot(attended, out_full, preferred_element_type=jnp.float32)
    second_scale = norm_scale(residual)
    hat_two = residual * second_scale
    normed_two = (hat_two * gain_two).astype(jnp.bfloat16)
    mlp_rows = lax.all_gather(normed_two, "tensor", axis=0, tiled=True)
    cot_rows = lax.all_gather(cotangent, "tensor", axis=0, tiled=True)
    gate_up = jnp.dot(mlp_rows, gate_up_full, preferred_element_type=jnp.float32)
    gate, up = gate_up[:, :hidden], gate_up[:, hidden:]
    sig = jax.nn.sigmoid(gate)
    act = (gate * sig * up).astype(jnp.bfloat16)
    d_act = jnp.dot(cot_rows, down_full, preferred_element_type=jnp.float32)
    d_gate = (d_act * up * sig * (1.0 + gate * (1.0 - sig))).astype(jnp.bfloat16)
    d_up = (d_act * gate * sig).astype(jnp.bfloat16)
    d_gate_up = jnp.concatenate([d_gate, d_up], axis=1)
    d_normed_two = lax.psum_scatter(
        lax.dot_general(
            d_gate_up, gate_up_full, COLS_MATCH, preferred_element_type=jnp.float32
        ).astype(jnp.bfloat16),
        "tensor",
        scatter_dimension=0,
        tiled=True,
    ).astype(jnp.float32)
    feed = lax.psum_scatter(
        lax.dot_general(act, down_full, COLS_MATCH, preferred_element_type=jnp.float32).astype(
            jnp.bfloat16
        ),
        "tensor",
        scatter_dimension=0,
        tiled=True,
    )
    output = (residual + feed.astype(jnp.float32)).astype(jnp.bfloat16)
    mlp_grads = jnp.concatenate(
        [
            lax.dot_general(mlp_rows, d_gate_up, ROWS_MATCH, preferred_element_type=jnp.float32),
            lax.dot_general(cot_rows, act, ROWS_MATCH, preferred_element_type=jnp.float32),
        ],
        axis=1,
    ).astype(jnp.bfloat16)

    mlp_gain_grad = jnp.sum(d_normed_two * hat_two, axis=0)
    d_residual = cotangent.astype(jnp.float32) + norm_back(
        d_normed_two, hat_two, second_scale, gain_two
    )
    residual_round = d_residual.astype(jnp.bfloat16)
    d_attended = lax.dot_general(
        residual_round, out_full, COLS_MATCH, preferred_element_type=jnp.float32
    ).astype(jnp.bfloat16)
    delta = jnp.sum(
        (d_attended.astype(jnp.float32) * attended.astype(jnp.float32)).reshape(rows, HEADS, HD),
        axis=-1,
    )
    delta = jnp.transpose(delta).reshape(KV_HEADS, 1, lanes)
    d_att_group = jnp.transpose(d_attended.reshape(rows, HEADS, HD), (1, 0, 2))
    d_att_pad = jnp.pad(d_att_group.reshape(KV_HEADS, lanes, HD), ((0, 0), (0, 0), (HD, 0)))
    dq_turned, dkv_terms = attend_backward(
        key_places, own_lanes, q_pad, d_att_pad, all_kv, totals, delta
    )
    own_dkv = lax.psum_scatter(dkv_terms, ("context", "tensor"), scatter_dimension=0)
    own_dkv = jnp.transpose(own_dkv.astype(jnp.float32), (1, 0, 2))
    d_query = jnp.transpose(dq_turned.reshape(KV_HEADS, HD, groups, rows), (3, 0, 2, 1)).reshape(
        rows, HEADS, HD
    )
    dq_rot = unrotate(d_query, cosine, sine).astype(jnp.bfloat16).reshape(rows, q_cols)
    dk_rot = unrotate(own_dkv[..., :HD], cosine, sine).astype(jnp.bfloat16).reshape(rows, kv_cols)
    dv_round = own_dkv[..., HD:].astype(jnp.bfloat16).reshape(rows, kv_cols)
    d_qkv = jnp.concatenate([dq_rot, dk_rot, dv_round], axis=1)
    d_normed_one = lax.dot_general(
        d_qkv, qkv_full, COLS_MATCH, preferred_element_type=jnp.float32
    )
    hat_one = inputs * first_scale
    attn_gain_grad = jnp.sum(d_normed_one * hat_one, axis=0)
    input_grad = d_residual + norm_back(d_normed_one, hat_one, first_scale, gain_one)

    parts = lax.axis_size("tensor")
    gathered_rows = lax.all_gather(
        jnp.concatenate([normed_one, attended], axis=1), "tensor", axis=0, tiled=True
    )
    quarters = jnp.concatenate(
        [
            piece.reshape(rows, parts, piece.shape[1] // parts)
            for piece in (dq_rot, dk_rot, dv_round, residual_round)
        ],
        axis=2,
    )
    own_cols = lax.all_to_all(quarters, "tensor", split_axis=1, concat_axis=0, tiled=True)
    own_cols = own_cols.reshape(parts * rows, quarters.shape[2])
    cut = qkv_cols // parts
    attn_grads = jnp.concatenate(
        [
            lax.dot_general(
                gathered_rows[:, :width],
                own_cols[:, :cut],
                ROWS_MATCH,
                preferred_element_type=jnp.float32,
            ),
            lax.dot_general(
                gathered_rows[:, width:],
                own_cols[:, cut:],
                ROWS_MATCH,
                preferred_element_type=jnp.float32,
            ),
            attn_gain_grad[:, None],
            mlp_gain_grad[:, None],
        ],
        axis=1,
    ).astype(jnp.bfloat16)

    mlp_share = lax.psum_scatter(
        mlp_grads, ("fsdp", "context"), scatter_dimension=0, tiled=True
    )
    mlp_owned = lax.all_gather(mlp_share, "context", axis=0, tiled=True).astype(jnp.float32)
    attn_share = lax.psum_scatter(
        attn_grads, ("fsdp", "context"), scatter_dimension=0, tiled=True
    )
    pieces = lax.all_gather(attn_share, ("context", "tensor"), axis=0)
    pieces = pieces.reshape(
        lax.axis_size("context"), parts, pieces.shape[1], pieces.shape[2]
    ).astype(jnp.float32)

    def whole(start, count):
        part = jnp.transpose(pieces[..., start : start + count], (0, 2, 1, 3))
        return part.reshape(part.shape[0] * part.shape[1], parts * count)

    q_part, kv_part = q_cols // parts, kv_cols // parts
    gains = jnp.sum(pieces[..., cut + width // parts :], axis=1).reshape(-1, 2)
    return (
        output,
        input_grad,
        gains[:, 0],
        whole(0, q_part),
        whole(q_part, kv_part),
        whole(q_part + kv_part, kv_part),
        whole(cut, width // parts),
        gains[:, 1],
        mlp_owned[:, :hidden],
        mlp_owned[:, hidden : 2 * hidden],
        mlp_owned[:, 2 * hidden :],
    )


def solution(mesh):
    return jax.shard_map(
        per_device,
        mesh=mesh,
        in_specs=(
            P(("fsdp", "context", "tensor"), None),
            P("fsdp", None),
            P(("fsdp", "context", "tensor"), None),
            P("fsdp"),
            P("fsdp", None),
            P("fsdp", None),
            P("fsdp", None),
            P("fsdp", None),
            P("fsdp"),
            P("fsdp", "tensor"),
            P("fsdp", "tensor"),
            P("fsdp", "tensor"),
        ),
        out_specs=(
            P(("fsdp", "context", "tensor"), None),
            P(("fsdp", "context", "tensor"), None),
            P("fsdp"),
            P("fsdp", None),
            P("fsdp", None),
            P("fsdp", None),
            P("fsdp", None),
            P("fsdp"),
            P("fsdp", "tensor"),
            P("fsdp", "tensor"),
            P("fsdp", "tensor"),
        ),
        check_vma=False,
    )
```

```python
import jax
import jax.numpy as jnp
from jax import lax
from jax.experimental import pallas as pl
from jax.experimental.pallas import tpu as pltpu
from jax.sharding import PartitionSpec as P

HEADS = 15
KV_HEADS = 5
HD = 64


EPS = 1e-05
THETA = 100000.0
NEG = -1e30
ROWS_MATCH = (((0,), (0,)), ((), ()))
COLS_MATCH = (((1,), (1,)), ((), ()))


def norm_scale(values):
    return lax.rsqrt(jnp.mean(values * values, axis=1, keepdims=True) + EPS)


def norm_back(grad, hat, scale, gain):
    weighted = grad * gain
    return scale * (weighted - hat * jnp.mean(weighted * hat, axis=1, keepdims=True))


def rotary_tables(places):
    half = HD // 2
    freq = THETA ** (-2.0 * jnp.arange(half, dtype=jnp.float32) / HD)
    angle = places.astype(jnp.float32)[:, None] * freq[None, :]
    cosine = jnp.concatenate([jnp.cos(angle), jnp.cos(angle)], axis=1)[:, None, :]
    sine = jnp.concatenate([jnp.sin(angle), jnp.sin(angle)], axis=1)[:, None, :]
    return (cosine, sine)


def rotate(values, cosine, sine):
    half = values.shape[-1] // 2
    turned = jnp.concatenate([-values[..., half:], values[..., :half]], axis=-1)
    return values * cosine + turned * sine


def unrotate(values, cosine, sine):
    half = values.shape[-1] // 2
    scaled = values * sine
    return values * cosine + jnp.concatenate([scaled[..., half:], -scaled[..., :half]], axis=-1)


KEYS_MATCH = (((0,), (0,)), ((), ()))


def masked_scores(kv, queries, key_places, own_places):
    scores = lax.dot_general(
        kv, queries, COLS_MATCH, preferred_element_type=jnp.float32
    ) * HD ** (-0.5)
    return jnp.where(key_places <= own_places, scores, NEG)


def forward_kernel(key_places_ref, own_places_ref, q_ref, kv_ref, out_ref, lse_ref):
    owners, _, block, width = kv_ref.shape
    kv = kv_ref[...].reshape(owners * block, width)
    scores = masked_scores(kv, q_ref[0], key_places_ref[...], own_places_ref[...])
    peak = jnp.max(scores, axis=0, keepdims=True)
    weights = jnp.exp(scores - peak)
    summed = jnp.sum(weights, axis=0, keepdims=True)
    mixed = lax.dot_general(
        kv, weights.astype(jnp.bfloat16), KEYS_MATCH, preferred_element_type=jnp.float32
    )
    out_ref[0] = (mixed[HD:] / summed).astype(jnp.bfloat16)
    lse_ref[0] = peak + jnp.log(summed)


def backward_kernel(
    key_places_ref, own_places_ref, q_ref, d_att_ref, kv_ref, lse_ref, delta_ref, dq_ref, dkv_ref
):
    owners, _, block, width = kv_ref.shape
    kv = kv_ref[...].reshape(owners * block, width)
    scores = masked_scores(kv, q_ref[0], key_places_ref[...], own_places_ref[...])
    probs = jnp.exp(scores - lse_ref[0])
    d_probs = lax.dot_general(kv, d_att_ref[0], COLS_MATCH, preferred_element_type=jnp.float32)
    d_scores = (probs * (d_probs - delta_ref[0]) * HD ** (-0.5)).astype(jnp.bfloat16)
    dq = lax.dot_general(kv, d_scores, KEYS_MATCH, preferred_element_type=jnp.float32)
    dq_ref[0] = dq[:HD]
    d_kv = jnp.dot(d_scores, q_ref[0], preferred_element_type=jnp.float32)
    d_kv = d_kv + jnp.dot(
        probs.astype(jnp.bfloat16), d_att_ref[0], preferred_element_type=jnp.float32
    )
    dkv_ref[...] = d_kv.astype(jnp.bfloat16).reshape(owners, 1, block, width)


def attention_specs(all_kv, lanes):
    owners, _, block, width = all_kv.shape
    total = owners * block
    places = pl.BlockSpec((total, 1), lambda g: (0, 0))
    own = pl.BlockSpec((1, lanes), lambda g: (0, 0))
    queries = pl.BlockSpec((1, lanes, width), lambda g: (g, 0, 0))
    kv = pl.BlockSpec((owners, 1, block, width), lambda g: (0, g, 0, 0))
    row = pl.BlockSpec((1, 1, lanes), lambda g: (g, 0, 0))
    turned = pl.BlockSpec((1, HD, lanes), lambda g: (g, 0, 0))
    cost = KV_HEADS * total * lanes
    return places, own, queries, kv, row, turned, cost


def attend_forward(key_places, own_lanes, q_pad, all_kv):
    lanes = q_pad.shape[1]
    places, own, queries, kv, row, turned, cost = attention_specs(all_kv, lanes)
    return pl.pallas_call(
        forward_kernel,
        grid=(KV_HEADS,),
        in_specs=[places, own, queries, kv],
        out_specs=[turned, row],
        out_shape=[
            jax.ShapeDtypeStruct((KV_HEADS, HD, lanes), jnp.bfloat16),
            jax.ShapeDtypeStruct((KV_HEADS, 1, lanes), jnp.float32),
        ],
        cost_estimate=pl.CostEstimate(
            flops=8 * HD * cost, bytes_accessed=2 * all_kv.size, transcendentals=cost
        ),
    )(key_places, own_lanes, q_pad, all_kv)


def attend_backward(key_places, own_lanes, q_pad, d_att_pad, all_kv, totals, delta):
    lanes = q_pad.shape[1]
    places, own, queries, kv, row, turned, cost = attention_specs(all_kv, lanes)
    return pl.pallas_call(
        backward_kernel,
        grid=(KV_HEADS,),
        in_specs=[places, own, queries, queries, kv, row, row],
        out_specs=[turned, kv],
        out_shape=[
            jax.ShapeDtypeStruct((KV_HEADS, HD, lanes), jnp.float32),
            jax.ShapeDtypeStruct(all_kv.shape, jnp.bfloat16),
        ],
        cost_estimate=pl.CostEstimate(
            flops=20 * HD * cost, bytes_accessed=4 * all_kv.size, transcendentals=cost
        ),
    )(key_places, own_lanes, q_pad, d_att_pad, all_kv, totals, delta)


def ring(axis):
    size = lax.axis_size(axis)
    return size, lax.axis_index(axis), [(i, (i + 1) % size) for i in range(size)]


def ring_gather(block, axis):
    size, me, hops = ring(axis)
    held = [block]
    for _ in range(size - 1):
        held.append(lax.ppermute(held[-1], axis, hops))
    ordered = [lax.select_n(lax.rem(me - j + size, size), *held) for j in range(size)]
    return held[-1], jnp.concatenate(ordered, axis=0)


def ring_reduce(values, axis):
    size, me, hops = ring(axis)
    count = values.shape[0] // size

    def block(step):
        which = lax.rem(me - 1 - step + 2 * size, size)
        return lax.dynamic_slice_in_dim(values, which * count, count, 0)

    total = block(0)
    for step in range(1, size):
        moved = lax.ppermute(total, axis, hops)
        total = (moved.astype(jnp.float32) + block(step).astype(jnp.float32)).astype(jnp.bfloat16)
    return total


def per_device(
    tokens,
    positions,
    cotangent,
    attn_gain,
    query_weight,
    key_weight,
    value_weight,
    out_weight,
    mlp_gain,
    gate_weight,
    up_weight,
    down_weight,
):
    rows, width = tokens.shape
    groups = HEADS // KV_HEADS
    lanes = groups * rows
    q_cols, kv_cols = query_weight.shape[1], key_weight.shape[1]
    qkv_cols = q_cols + 2 * kv_cols
    hidden = gate_weight.shape[1]
    place = lax.axis_index(("context", "tensor"))
    sequence_places = positions[0]
    own_places = lax.dynamic_slice_in_dim(sequence_places, place * rows, rows, 0)
    key_places = sequence_places[:, None]
    own_lanes = jnp.tile(own_places, groups)[None, :]

    last_block, first_pack = ring_gather(
        jnp.concatenate(
            [query_weight, key_weight, value_weight, attn_gain[:, None], mlp_gain[:, None]], axis=1
        ),
        "fsdp",
    )
    qkv_full = first_pack[:, :qkv_cols]
    gain_one = first_pack[:, qkv_cols].astype(jnp.float32)
    gain_two = first_pack[:, qkv_cols + 1].astype(jnp.float32)
    second_block, _ = lax.optimization_barrier(
        (
            jnp.concatenate([gate_weight, up_weight, down_weight, out_weight], axis=1),
            last_block,
        )
    )
    _, second_pack = ring_gather(second_block, "fsdp")
    gate_up_full = second_pack[:, : 2 * hidden]
    down_full = second_pack[:, 2 * hidden : 3 * hidden]
    out_full = second_pack[:, 3 * hidden :]

    inputs = tokens.astype(jnp.float32)
    first_scale = norm_scale(inputs)
    normed_one = (inputs * first_scale * gain_one).astype(jnp.bfloat16)
    cosine, sine = rotary_tables(own_places)
    qkv = jnp.dot(normed_one, qkv_full, preferred_element_type=jnp.float32)
    query = qkv[:, :q_cols].reshape(rows, HEADS, HD)
    key_raw = qkv[:, q_cols : q_cols + kv_cols].reshape(rows, KV_HEADS, HD)
    value = qkv[:, q_cols + kv_cols :].reshape(rows, KV_HEADS, HD).astype(jnp.bfloat16)
    q_rot = rotate(query, cosine, sine).astype(jnp.bfloat16)
    k_rot = rotate(key_raw, cosine, sine).astype(jnp.bfloat16)
    own_kv = jnp.transpose(jnp.concatenate([k_rot, value], axis=2), (1, 0, 2))
    all_kv = lax.all_gather(own_kv, ("context", "tensor"), axis=0)
    q_group = jnp.transpose(q_rot, (1, 0, 2)).reshape(KV_HEADS, lanes, HD)
    q_pad = jnp.pad(q_group, ((0, 0), (0, 0), (0, HD)))
    turned, totals = attend_forward(key_places, own_lanes, q_pad, all_kv)
    attended = jnp.transpose(
        turned.reshape(KV_HEADS, HD, groups, rows), (3, 0, 2, 1)
    ).reshape(rows, HEADS * HD)

    residual = inputs + jnp.dot(attended, out_full, preferred_element_type=jnp.float32)
    second_scale = norm_scale(residual)
    hat_two = residual * second_scale
    normed_two = (hat_two * gain_two).astype(jnp.bfloat16)
    mlp_rows = lax.all_gather(normed_two, "tensor", axis=0, tiled=True)
    cot_rows = lax.all_gather(cotangent, "tensor", axis=0, tiled=True)
    gate_up = jnp.dot(mlp_rows, gate_up_full, preferred_element_type=jnp.float32)
    gate, up = gate_up[:, :hidden], gate_up[:, hidden:]
    sig = jax.nn.sigmoid(gate)
    act = (gate * sig * up).astype(jnp.bfloat16)
    d_act = jnp.dot(cot_rows, down_full, preferred_element_type=jnp.float32)
    d_gate = (d_act * up * sig * (1.0 + gate * (1.0 - sig))).astype(jnp.bfloat16)
    d_up = (d_act * gate * sig).astype(jnp.bfloat16)
    d_gate_up = jnp.concatenate([d_gate, d_up], axis=1)
    d_normed_two = lax.psum_scatter(
        lax.dot_general(
            d_gate_up, gate_up_full, COLS_MATCH, preferred_element_type=jnp.float32
        ).astype(jnp.bfloat16),
        "tensor",
        scatter_dimension=0,
        tiled=True,
    ).astype(jnp.float32)
    feed = lax.psum_scatter(
        lax.dot_general(act, down_full, COLS_MATCH, preferred_element_type=jnp.float32).astype(
            jnp.bfloat16
        ),
        "tensor",
        scatter_dimension=0,
        tiled=True,
    )
    output = (residual + feed.astype(jnp.float32)).astype(jnp.bfloat16)
    mlp_grads = jnp.concatenate(
        [
            lax.dot_general(mlp_rows, d_gate_up, ROWS_MATCH, preferred_element_type=jnp.float32),
            lax.dot_general(cot_rows, act, ROWS_MATCH, preferred_element_type=jnp.float32),
        ],
        axis=1,
    ).astype(jnp.bfloat16)

    mlp_gain_grad = jnp.sum(d_normed_two * hat_two, axis=0)
    d_residual = cotangent.astype(jnp.float32) + norm_back(
        d_normed_two, hat_two, second_scale, gain_two
    )
    residual_round = d_residual.astype(jnp.bfloat16)
    d_attended = lax.dot_general(
        residual_round, out_full, COLS_MATCH, preferred_element_type=jnp.float32
    ).astype(jnp.bfloat16)
    delta = jnp.sum(
        (d_attended.astype(jnp.float32) * attended.astype(jnp.float32)).reshape(rows, HEADS, HD),
        axis=-1,
    )
    delta = jnp.transpose(delta).reshape(KV_HEADS, 1, lanes)
    d_att_group = jnp.transpose(d_attended.reshape(rows, HEADS, HD), (1, 0, 2))
    d_att_pad = jnp.pad(d_att_group.reshape(KV_HEADS, lanes, HD), ((0, 0), (0, 0), (HD, 0)))
    dq_turned, dkv_terms = attend_backward(
        key_places, own_lanes, q_pad, d_att_pad, all_kv, totals, delta
    )
    own_dkv = lax.psum_scatter(dkv_terms, ("context", "tensor"), scatter_dimension=0)
    own_dkv = jnp.transpose(own_dkv.astype(jnp.float32), (1, 0, 2))
    d_query = jnp.transpose(dq_turned.reshape(KV_HEADS, HD, groups, rows), (3, 0, 2, 1)).reshape(
        rows, HEADS, HD
    )
    dq_rot = unrotate(d_query, cosine, sine).astype(jnp.bfloat16).reshape(rows, q_cols)
    dk_rot = unrotate(own_dkv[..., :HD], cosine, sine).astype(jnp.bfloat16).reshape(rows, kv_cols)
    dv_round = own_dkv[..., HD:].astype(jnp.bfloat16).reshape(rows, kv_cols)
    d_qkv = jnp.concatenate([dq_rot, dk_rot, dv_round], axis=1)
    d_normed_one = lax.dot_general(
        d_qkv, qkv_full, COLS_MATCH, preferred_element_type=jnp.float32
    )
    hat_one = inputs * first_scale
    attn_gain_grad = jnp.sum(d_normed_one * hat_one, axis=0)
    input_grad = d_residual + norm_back(d_normed_one, hat_one, first_scale, gain_one)

    parts = lax.axis_size("tensor")
    gathered_rows = lax.all_gather(
        jnp.concatenate([normed_one, attended], axis=1), "tensor", axis=0, tiled=True
    )
    quarters = jnp.concatenate(
        [
            piece.reshape(rows, parts, piece.shape[1] // parts)
            for piece in (dq_rot, dk_rot, dv_round, residual_round)
        ],
        axis=2,
    )
    own_cols = lax.all_to_all(quarters, "tensor", split_axis=1, concat_axis=0, tiled=True)
    own_cols = own_cols.reshape(parts * rows, quarters.shape[2])
    cut = qkv_cols // parts
    attn_grads = jnp.concatenate(
        [
            lax.dot_general(
                gathered_rows[:, :width],
                own_cols[:, :cut],
                ROWS_MATCH,
                preferred_element_type=jnp.float32,
            ),
            lax.dot_general(
                gathered_rows[:, width:],
                own_cols[:, cut:],
                ROWS_MATCH,
                preferred_element_type=jnp.float32,
            ),
            attn_gain_grad[:, None],
            mlp_gain_grad[:, None],
        ],
        axis=1,
    ).astype(jnp.bfloat16)

    mlp_share = lax.psum_scatter(
        ring_reduce(mlp_grads, "fsdp"), "context", scatter_dimension=0, tiled=True
    )
    mlp_owned = lax.all_gather(mlp_share, "context", axis=0, tiled=True).astype(jnp.float32)
    attn_share = lax.psum_scatter(
        ring_reduce(attn_grads, "fsdp"), "context", scatter_dimension=0, tiled=True
    )
    pieces = lax.all_gather(attn_share, ("context", "tensor"), axis=0)
    pieces = pieces.reshape(
        lax.axis_size("context"), parts, pieces.shape[1], pieces.shape[2]
    ).astype(jnp.float32)

    def whole(start, count):
        part = jnp.transpose(pieces[..., start : start + count], (0, 2, 1, 3))
        return part.reshape(part.shape[0] * part.shape[1], parts * count)

    q_part, kv_part = q_cols // parts, kv_cols // parts
    gains = jnp.sum(pieces[..., cut + width // parts :], axis=1).reshape(-1, 2)
    return (
        output,
        input_grad,
        gains[:, 0],
        whole(0, q_part),
        whole(q_part, kv_part),
        whole(q_part + kv_part, kv_part),
        whole(cut, width // parts),
        gains[:, 1],
        mlp_owned[:, :hidden],
        mlp_owned[:, hidden : 2 * hidden],
        mlp_owned[:, 2 * hidden :],
    )


def solution(mesh):
    return jax.shard_map(
        per_device,
        mesh=mesh,
        in_specs=(
            P(("fsdp", "context", "tensor"), None),
            P("fsdp", None),
            P(("fsdp", "context", "tensor"), None),
            P("fsdp"),
            P("fsdp", None),
            P("fsdp", None),
            P("fsdp", None),
            P("fsdp", None),
            P("fsdp"),
            P("fsdp", "tensor"),
            P("fsdp", "tensor"),
            P("fsdp", "tensor"),
        ),
        out_specs=(
            P(("fsdp", "context", "tensor"), None),
            P(("fsdp", "context", "tensor"), None),
            P("fsdp"),
            P("fsdp", None),
            P("fsdp", None),
            P("fsdp", None),
            P("fsdp", None),
            P("fsdp"),
            P("fsdp", "tensor"),
            P("fsdp", "tensor"),
            P("fsdp", "tensor"),
        ),
        check_vma=False,
    )
```

```python
import jax
import jax.numpy as jnp
from jax import lax
from jax.experimental import pallas as pl
from jax.experimental.pallas import tpu as pltpu
from jax.sharding import PartitionSpec as P

HEADS = 15
KV_HEADS = 5
HD = 64


EPS = 1e-05
THETA = 100000.0
NEG = -1e30
ROWS_MATCH = (((0,), (0,)), ((), ()))
COLS_MATCH = (((1,), (1,)), ((), ()))


def norm_scale(values):
    return lax.rsqrt(jnp.mean(values * values, axis=1, keepdims=True) + EPS)


def norm_back(grad, hat, scale, gain):
    weighted = grad * gain
    return scale * (weighted - hat * jnp.mean(weighted * hat, axis=1, keepdims=True))


def rotary_tables(places):
    half = HD // 2
    freq = THETA ** (-2.0 * jnp.arange(half, dtype=jnp.float32) / HD)
    angle = places.astype(jnp.float32)[:, None] * freq[None, :]
    cosine = jnp.concatenate([jnp.cos(angle), jnp.cos(angle)], axis=1)[:, None, :]
    sine = jnp.concatenate([jnp.sin(angle), jnp.sin(angle)], axis=1)[:, None, :]
    return (cosine, sine)


def rotate(values, cosine, sine):
    half = values.shape[-1] // 2
    turned = jnp.concatenate([-values[..., half:], values[..., :half]], axis=-1)
    return values * cosine + turned * sine


def unrotate(values, cosine, sine):
    half = values.shape[-1] // 2
    scaled = values * sine
    return values * cosine + jnp.concatenate([scaled[..., half:], -scaled[..., :half]], axis=-1)


KEYS_MATCH = (((0,), (0,)), ((), ()))


def masked_scores(kv, queries, key_places, own_places):
    scores = lax.dot_general(
        kv, queries, COLS_MATCH, preferred_element_type=jnp.float32
    ) * HD ** (-0.5)
    return jnp.where(key_places <= own_places, scores, NEG)


def forward_kernel(key_places_ref, own_places_ref, q_ref, kv_ref, out_ref, lse_ref):
    owners, _, block, width = kv_ref.shape
    kv = kv_ref[...].reshape(owners * block, width)
    scores = masked_scores(kv, q_ref[0], key_places_ref[...], own_places_ref[...])
    peak = jnp.max(scores, axis=0, keepdims=True)
    weights = jnp.exp(scores - peak)
    summed = jnp.sum(weights, axis=0, keepdims=True)
    mixed = lax.dot_general(
        kv, weights.astype(jnp.bfloat16), KEYS_MATCH, preferred_element_type=jnp.float32
    )
    out_ref[0] = (mixed[HD:] / summed).astype(jnp.bfloat16)
    lse_ref[0] = peak + jnp.log(summed)


def backward_kernel(
    key_places_ref, own_places_ref, q_ref, d_att_ref, kv_ref, lse_ref, delta_ref, dq_ref, dkv_ref
):
    owners, _, block, width = kv_ref.shape
    kv = kv_ref[...].reshape(owners * block, width)
    scores = masked_scores(kv, q_ref[0], key_places_ref[...], own_places_ref[...])
    probs = jnp.exp(scores - lse_ref[0])
    d_probs = lax.dot_general(kv, d_att_ref[0], COLS_MATCH, preferred_element_type=jnp.float32)
    d_scores = (probs * (d_probs - delta_ref[0]) * HD ** (-0.5)).astype(jnp.bfloat16)
    dq = lax.dot_general(kv, d_scores, KEYS_MATCH, preferred_element_type=jnp.float32)
    dq_ref[0] = dq[:HD]
    d_kv = jnp.dot(d_scores, q_ref[0], preferred_element_type=jnp.float32)
    d_kv = d_kv + jnp.dot(
        probs.astype(jnp.bfloat16), d_att_ref[0], preferred_element_type=jnp.float32
    )
    dkv_ref[...] = d_kv.astype(jnp.bfloat16).reshape(owners, 1, block, width)


def attention_specs(all_kv, lanes):
    owners, _, block, width = all_kv.shape
    total = owners * block
    places = pl.BlockSpec((total, 1), lambda g: (0, 0))
    own = pl.BlockSpec((1, lanes), lambda g: (0, 0))
    queries = pl.BlockSpec((1, lanes, width), lambda g: (g, 0, 0))
    kv = pl.BlockSpec((owners, 1, block, width), lambda g: (0, g, 0, 0))
    row = pl.BlockSpec((1, 1, lanes), lambda g: (g, 0, 0))
    turned = pl.BlockSpec((1, HD, lanes), lambda g: (g, 0, 0))
    cost = KV_HEADS * total * lanes
    return places, own, queries, kv, row, turned, cost


def attend_forward(key_places, own_lanes, q_pad, all_kv):
    lanes = q_pad.shape[1]
    places, own, queries, kv, row, turned, cost = attention_specs(all_kv, lanes)
    return pl.pallas_call(
        forward_kernel,
        grid=(KV_HEADS,),
        in_specs=[places, own, queries, kv],
        out_specs=[turned, row],
        out_shape=[
            jax.ShapeDtypeStruct((KV_HEADS, HD, lanes), jnp.bfloat16),
            jax.ShapeDtypeStruct((KV_HEADS, 1, lanes), jnp.float32),
        ],
        cost_estimate=pl.CostEstimate(
            flops=8 * HD * cost, bytes_accessed=2 * all_kv.size, transcendentals=cost
        ),
    )(key_places, own_lanes, q_pad, all_kv)


def attend_backward(key_places, own_lanes, q_pad, d_att_pad, all_kv, totals, delta):
    lanes = q_pad.shape[1]
    places, own, queries, kv, row, turned, cost = attention_specs(all_kv, lanes)
    return pl.pallas_call(
        backward_kernel,
        grid=(KV_HEADS,),
        in_specs=[places, own, queries, queries, kv, row, row],
        out_specs=[turned, kv],
        out_shape=[
            jax.ShapeDtypeStruct((KV_HEADS, HD, lanes), jnp.float32),
            jax.ShapeDtypeStruct(all_kv.shape, jnp.bfloat16),
        ],
        cost_estimate=pl.CostEstimate(
            flops=20 * HD * cost, bytes_accessed=4 * all_kv.size, transcendentals=cost
        ),
    )(key_places, own_lanes, q_pad, d_att_pad, all_kv, totals, delta)


def ring(axis):
    size = lax.axis_size(axis)
    return size, lax.axis_index(axis), [(i, (i + 1) % size) for i in range(size)]


def ring_gather(block, axis):
    size, me, hops = ring(axis)
    held = [block]
    for _ in range(size - 1):
        held.append(lax.ppermute(held[-1], axis, hops))
    ordered = [lax.select_n(lax.rem(me - j + size, size), *held) for j in range(size)]
    return held[-1], jnp.concatenate(ordered, axis=0)


def ring_reduce(values, axis):
    size, me, hops = ring(axis)
    count = values.shape[0] // size

    def block(step):
        which = lax.rem(me - 1 - step + 2 * size, size)
        return lax.dynamic_slice_in_dim(values, which * count, count, 0)

    total = block(0)
    for step in range(1, size):
        moved = lax.ppermute(total, axis, hops)
        total = (moved.astype(jnp.float32) + block(step).astype(jnp.float32)).astype(jnp.bfloat16)
    return total


def per_device(
    tokens,
    positions,
    cotangent,
    attn_gain,
    query_weight,
    key_weight,
    value_weight,
    out_weight,
    mlp_gain,
    gate_weight,
    up_weight,
    down_weight,
):
    rows, width = tokens.shape
    groups = HEADS // KV_HEADS
    lanes = groups * rows
    q_cols, kv_cols = query_weight.shape[1], key_weight.shape[1]
    qkv_cols = q_cols + 2 * kv_cols
    hidden = gate_weight.shape[1]
    place = lax.axis_index(("context", "tensor"))
    sequence_places = positions[0]
    own_places = lax.dynamic_slice_in_dim(sequence_places, place * rows, rows, 0)
    key_places = sequence_places[:, None]
    own_lanes = jnp.tile(own_places, groups)[None, :]

    last_block, first_pack = ring_gather(
        jnp.concatenate(
            [query_weight, key_weight, value_weight, attn_gain[:, None], mlp_gain[:, None]], axis=1
        ),
        "fsdp",
    )
    qkv_full = first_pack[:, :qkv_cols]
    gain_one = first_pack[:, qkv_cols].astype(jnp.float32)
    gain_two = first_pack[:, qkv_cols + 1].astype(jnp.float32)
    second_block, _ = lax.optimization_barrier(
        (
            jnp.concatenate([gate_weight, up_weight, down_weight, out_weight], axis=1),
            last_block,
        )
    )
    _, second_pack = ring_gather(second_block, "fsdp")
    gate_up_full = second_pack[:, : 2 * hidden]
    down_full = second_pack[:, 2 * hidden : 3 * hidden]
    out_full = second_pack[:, 3 * hidden :]

    inputs = tokens.astype(jnp.float32)
    first_scale = norm_scale(inputs)
    normed_one = (inputs * first_scale * gain_one).astype(jnp.bfloat16)
    cosine, sine = rotary_tables(own_places)
    qkv = jnp.dot(normed_one, qkv_full, preferred_element_type=jnp.float32)
    query = qkv[:, :q_cols].reshape(rows, HEADS, HD)
    key_raw = qkv[:, q_cols : q_cols + kv_cols].reshape(rows, KV_HEADS, HD)
    value = qkv[:, q_cols + kv_cols :].reshape(rows, KV_HEADS, HD).astype(jnp.bfloat16)
    q_rot = rotate(query, cosine, sine).astype(jnp.bfloat16)
    k_rot = rotate(key_raw, cosine, sine).astype(jnp.bfloat16)
    own_kv = jnp.transpose(jnp.concatenate([k_rot, value], axis=2), (1, 0, 2))
    all_kv = lax.all_gather(own_kv, ("context", "tensor"), axis=0)
    q_group = jnp.transpose(q_rot, (1, 0, 2)).reshape(KV_HEADS, lanes, HD)
    q_pad = jnp.pad(q_group, ((0, 0), (0, 0), (0, HD)))
    turned, totals = attend_forward(key_places, own_lanes, q_pad, all_kv)
    attended = jnp.transpose(
        turned.reshape(KV_HEADS, HD, groups, rows), (3, 0, 2, 1)
    ).reshape(rows, HEADS * HD)

    residual = inputs + jnp.dot(attended, out_full, preferred_element_type=jnp.float32)
    second_scale = norm_scale(residual)
    hat_two = residual * second_scale
    normed_two = (hat_two * gain_two).astype(jnp.bfloat16)
    mlp_rows = lax.all_gather(normed_two, "tensor", axis=0, tiled=True)
    cot_rows = lax.all_gather(cotangent, "tensor", axis=0, tiled=True)
    gate_up = jnp.dot(mlp_rows, gate_up_full, preferred_element_type=jnp.float32)
    gate, up = gate_up[:, :hidden], gate_up[:, hidden:]
    sig = jax.nn.sigmoid(gate)
    act = (gate * sig * up).astype(jnp.bfloat16)
    d_act = jnp.dot(cot_rows, down_full, preferred_element_type=jnp.float32)
    d_gate = (d_act * up * sig * (1.0 + gate * (1.0 - sig))).astype(jnp.bfloat16)
    d_up = (d_act * gate * sig).astype(jnp.bfloat16)
    d_gate_up = jnp.concatenate([d_gate, d_up], axis=1)
    d_normed_two = ring_reduce(
        lax.dot_general(
            d_gate_up, gate_up_full, COLS_MATCH, preferred_element_type=jnp.float32
        ).astype(jnp.bfloat16),
        "tensor",
    ).astype(jnp.float32)
    feed = ring_reduce(
        lax.dot_general(act, down_full, COLS_MATCH, preferred_element_type=jnp.float32).astype(
            jnp.bfloat16
        ),
        "tensor",
    )
    output = (residual + feed.astype(jnp.float32)).astype(jnp.bfloat16)
    mlp_grads = jnp.concatenate(
        [
            lax.dot_general(mlp_rows, d_gate_up, ROWS_MATCH, preferred_element_type=jnp.float32),
            lax.dot_general(cot_rows, act, ROWS_MATCH, preferred_element_type=jnp.float32),
        ],
        axis=1,
    ).astype(jnp.bfloat16)

    mlp_gain_grad = jnp.sum(d_normed_two * hat_two, axis=0)
    d_residual = cotangent.astype(jnp.float32) + norm_back(
        d_normed_two, hat_two, second_scale, gain_two
    )
    residual_round = d_residual.astype(jnp.bfloat16)
    d_attended = lax.dot_general(
        residual_round, out_full, COLS_MATCH, preferred_element_type=jnp.float32
    ).astype(jnp.bfloat16)
    delta = jnp.sum(
        (d_attended.astype(jnp.float32) * attended.astype(jnp.float32)).reshape(rows, HEADS, HD),
        axis=-1,
    )
    delta = jnp.transpose(delta).reshape(KV_HEADS, 1, lanes)
    d_att_group = jnp.transpose(d_attended.reshape(rows, HEADS, HD), (1, 0, 2))
    d_att_pad = jnp.pad(d_att_group.reshape(KV_HEADS, lanes, HD), ((0, 0), (0, 0), (HD, 0)))
    dq_turned, dkv_terms = attend_backward(
        key_places, own_lanes, q_pad, d_att_pad, all_kv, totals, delta
    )
    own_dkv = lax.psum_scatter(dkv_terms, ("context", "tensor"), scatter_dimension=0)
    own_dkv = jnp.transpose(own_dkv.astype(jnp.float32), (1, 0, 2))
    d_query = jnp.transpose(dq_turned.reshape(KV_HEADS, HD, groups, rows), (3, 0, 2, 1)).reshape(
        rows, HEADS, HD
    )
    dq_rot = unrotate(d_query, cosine, sine).astype(jnp.bfloat16).reshape(rows, q_cols)
    dk_rot = unrotate(own_dkv[..., :HD], cosine, sine).astype(jnp.bfloat16).reshape(rows, kv_cols)
    dv_round = own_dkv[..., HD:].astype(jnp.bfloat16).reshape(rows, kv_cols)
    d_qkv = jnp.concatenate([dq_rot, dk_rot, dv_round], axis=1)
    d_normed_one = lax.dot_general(
        d_qkv, qkv_full, COLS_MATCH, preferred_element_type=jnp.float32
    )
    hat_one = inputs * first_scale
    attn_gain_grad = jnp.sum(d_normed_one * hat_one, axis=0)
    input_grad = d_residual + norm_back(d_normed_one, hat_one, first_scale, gain_one)

    parts = lax.axis_size("tensor")
    gathered_rows = lax.all_gather(
        jnp.concatenate([normed_one, attended], axis=1), "tensor", axis=0, tiled=True
    )
    quarters = jnp.concatenate(
        [
            piece.reshape(rows, parts, piece.shape[1] // parts)
            for piece in (dq_rot, dk_rot, dv_round, residual_round)
        ],
        axis=2,
    )
    own_cols = lax.all_to_all(quarters, "tensor", split_axis=1, concat_axis=0, tiled=True)
    own_cols = own_cols.reshape(parts * rows, quarters.shape[2])
    cut = qkv_cols // parts
    attn_grads = jnp.concatenate(
        [
            lax.dot_general(
                gathered_rows[:, :width],
                own_cols[:, :cut],
                ROWS_MATCH,
                preferred_element_type=jnp.float32,
            ),
            lax.dot_general(
                gathered_rows[:, width:],
                own_cols[:, cut:],
                ROWS_MATCH,
                preferred_element_type=jnp.float32,
            ),
            attn_gain_grad[:, None],
            mlp_gain_grad[:, None],
        ],
        axis=1,
    ).astype(jnp.bfloat16)

    mlp_share = lax.psum_scatter(
        ring_reduce(mlp_grads, "fsdp"), "context", scatter_dimension=0, tiled=True
    )
    mlp_owned = lax.all_gather(mlp_share, "context", axis=0, tiled=True).astype(jnp.float32)
    attn_share = lax.psum_scatter(
        ring_reduce(attn_grads, "fsdp"), "context", scatter_dimension=0, tiled=True
    )
    pieces = lax.all_gather(attn_share, ("context", "tensor"), axis=0)
    pieces = pieces.reshape(
        lax.axis_size("context"), parts, pieces.shape[1], pieces.shape[2]
    ).astype(jnp.float32)

    def whole(start, count):
        part = jnp.transpose(pieces[..., start : start + count], (0, 2, 1, 3))
        return part.reshape(part.shape[0] * part.shape[1], parts * count)

    q_part, kv_part = q_cols // parts, kv_cols // parts
    gains = jnp.sum(pieces[..., cut + width // parts :], axis=1).reshape(-1, 2)
    return (
        output,
        input_grad,
        gains[:, 0],
        whole(0, q_part),
        whole(q_part, kv_part),
        whole(q_part + kv_part, kv_part),
        whole(cut, width // parts),
        gains[:, 1],
        mlp_owned[:, :hidden],
        mlp_owned[:, hidden : 2 * hidden],
        mlp_owned[:, 2 * hidden :],
    )


def solution(mesh):
    return jax.shard_map(
        per_device,
        mesh=mesh,
        in_specs=(
            P(("fsdp", "context", "tensor"), None),
            P("fsdp", None),
            P(("fsdp", "context", "tensor"), None),
            P("fsdp"),
            P("fsdp", None),
            P("fsdp", None),
            P("fsdp", None),
            P("fsdp", None),
            P("fsdp"),
            P("fsdp", "tensor"),
            P("fsdp", "tensor"),
            P("fsdp", "tensor"),
        ),
        out_specs=(
            P(("fsdp", "context", "tensor"), None),
            P(("fsdp", "context", "tensor"), None),
            P("fsdp"),
            P("fsdp", None),
            P("fsdp", None),
            P("fsdp", None),
            P("fsdp", None),
            P("fsdp"),
            P("fsdp", "tensor"),
            P("fsdp", "tensor"),
            P("fsdp", "tensor"),
        ),
        check_vma=False,
    )
```
